32 devices in a mesh: rep: 4 (over y, core), dp: 8 (over z, x).
Axes of the slice: x: 2, y: 2, z: 4, core: 2. Of those that a mesh axis runs over, the one named last changes fastest.
Arguments:
- query_states: bfloat16 [256, 32, 768], P(('rep', 'dp')), may hold values from -12 to 12
- passage_states: bfloat16 [128, 180, 768], P(('rep', 'dp')), may hold values from -12 to 12
- query_lengths: int32 [256], P(('rep', 'dp')), may hold values from 8 to 32, as said below
- passage_lengths: int32 [128], P(('rep', 'dp')), may hold values from 45 to 180, as said below
- passage_ids: int32 [128, 180], P(('rep', 'dp')), may hold values from 2 to 30521, as said below
- positives: int32 [256], P(('rep', 'dp')), may hold values from 0 to 31, as said below
- up_weight: bfloat16 [768, 3072], replicated, may hold values from -0.21875 to 0.21875
- up_bias: float32 [3072], replicated, may hold values from -3 to 3
- down_weight: bfloat16 [3072, 768], replicated, may hold values from -0.109375 to 0.109375
- down_bias: float32 [768], replicated, may hold values from -3 to 3
- norm_gain: float32 [768], replicated, may hold values from 0.5 to 1.5
- norm_bias: float32 [768], replicated, may hold values from -2 to 2
- proj_weight: bfloat16 [768, 128], replicated, may hold values from -0.21875 to 0.21875
Outputs:
- mean_loss: float32 [], replicated
- passage_grad: float32 [128, 180, 128], P(('rep', 'dp'))
- proj_grad: float32 [768, 128], replicated
The draws below stay inside these ranges and needn't reach their ends.
Inputs may be any that keep to these rules, and one draw needn't show every extreme that they name: `query_lengths`: every device holds a query with all 32 slots real. `passage_lengths`: every device holds a passage with all 180 slots real. `passage_ids`: slots 0 and 1 of every passage hold ids 101 and 2; ids 999 to 1066 are punctuation. `positives`: index of the positive passage among the 32 passages of the query's replica group, in the order of the devices.
All inputs are finite; a program needn't handle non-finite values.
Results may differ from the reference program's by a relative error of at most 0.0055.
Values may be sent and summed in bfloat16 or wider, within the bound.
A program may use at most 128 MiB of HBM per device.

```python
import jax
import jax.numpy as jnp
from jax import lax

D = 768
FF = 3072
EMB = 128
QLEN = 32
PLEN = 180
Q_DEV = 8
P_DEV = 4
GROUP_Q = 64
GROUP_P = 32
QUERIES = 256
PASSAGES = 128
N_REP = 4
N_DP = 8


vocab_top = 30522


punct_low = 999


punct_high = 1067


def integer_tables(key):
    folded = jax.random.fold_in(key, 4711)
    subkeys = jax.random.split(folded, 9)
    pass_lengths = jax.random.randint(subkeys[0], (PASSAGES,), PLEN // 4, PLEN + 1)
    pass_full = jax.random.randint(subkeys[1], (PASSAGES // P_DEV,), 0, P_DEV)
    pass_mark = (jnp.arange(P_DEV)[None, :] == pass_full[:, None]).reshape(PASSAGES)
    pass_lengths = jnp.where(pass_mark, PLEN, pass_lengths).astype(jnp.int32)
    query_lengths = jax.random.randint(subkeys[2], (QUERIES,), QLEN // 4, QLEN + 1)
    query_full = jax.random.randint(subkeys[3], (QUERIES // Q_DEV,), 0, Q_DEV)
    query_mark = (jnp.arange(Q_DEV)[None, :] == query_full[:, None]).reshape(QUERIES)
    query_lengths = jnp.where(query_mark, QLEN, query_lengths).astype(jnp.int32)
    is_punct = jax.random.randint(subkeys[4], (PASSAGES, PLEN), 0, 100) < 15
    punct_ids = jax.random.randint(subkeys[5], (PASSAGES, PLEN), punct_low, punct_high)
    word_ids = jax.random.randint(subkeys[6], (PASSAGES, PLEN), 1999, vocab_top)
    token_ids = jnp.where(is_punct, punct_ids, word_ids)
    column = jnp.arange(PLEN)[None, :]
    token_ids = jnp.where(column == 0, 101, jnp.where(column == 1, 2, token_ids)).astype(jnp.int32)
    positives = jax.random.randint(subkeys[7], (QUERIES,), 0, GROUP_P).astype(jnp.int32)
    return (query_lengths, pass_lengths, token_ids, positives)


def passage_tables(key):
    folded = jax.random.fold_in(key, 5813)
    subkeys = jax.random.split(folded, 3)
    states = jax.random.normal(subkeys[0], (PASSAGES, PLEN, D), jnp.float32)
    return jnp.clip(states, -12.0, 12.0)


def draw_passage_states(key, part):
    return passage_tables(key).astype(jnp.bfloat16)


def draw_query_states(key, part):
    query_lengths, pass_lengths, token_ids, positives = integer_tables(key)
    states = passage_tables(key)
    folded = jax.random.fold_in(key, 6907)
    subkeys = jax.random.split(folded, 4)
    group_index = jnp.arange(QUERIES) // GROUP_Q
    target = group_index * GROUP_P + positives
    pick_pos = jax.random.randint(subkeys[0], (QUERIES, QLEN), 0, 1 << 20) % pass_lengths[target][:, None]
    copied = states[target[:, None], pick_pos]
    noise_part = jax.random.normal(subkeys[1], (QUERIES, QLEN, D), jnp.float32)
    copy_flag = jax.random.randint(subkeys[2], (QUERIES, QLEN), 0, 2) == 1
    blended = jnp.where(copy_flag[:, :, None], 0.7 * copied + 0.7 * noise_part, noise_part)
    return jnp.clip(blended, -12.0, 12.0).astype(jnp.bfloat16)


def draw_query_lengths(key, part):
    return integer_tables(key)[0]


def draw_passage_lengths(key, part):
    return integer_tables(key)[1]


def draw_passage_ids(key, part):
    return integer_tables(key)[2]


def draw_positives(key, part):
    return integer_tables(key)[3]


def scatter_about(rng, extent, deviation, limit, held_as=jnp.bfloat16):
    values = deviation * jax.random.normal(rng, extent, jnp.float32)
    return jnp.clip(values, min=-limit, max=limit).astype(held_as)


def setup_inputs(seed: int = 0) -> dict:
    keys = jax.random.split(jax.random.key(seed), 14)
    query_states = draw_query_states(jax.random.fold_in(keys[13], 71), 0)
    passage_states = draw_passage_states(jax.random.fold_in(keys[13], 71), 0)
    query_lengths = draw_query_lengths(jax.random.fold_in(keys[13], 71), 0)
    passage_lengths = draw_passage_lengths(jax.random.fold_in(keys[13], 71), 0)
    passage_ids = draw_passage_ids(jax.random.fold_in(keys[13], 71), 0)
    positives = draw_positives(jax.random.fold_in(keys[13], 71), 0)
    up_weight = scatter_about(keys[6], (D, FF), D ** -0.5, 0.21875)
    up_bias = scatter_about(keys[7], (FF,), 0.5, 3.0, jnp.float32)
    down_weight = scatter_about(keys[8], (FF, D), FF ** -0.5, 0.109375)
    down_bias = scatter_about(keys[9], (D,), 0.5, 3.0, jnp.float32)
    norm_gain = jnp.clip(1.0 + 0.1 * jax.random.normal(keys[10], (D,), jnp.float32), 0.5, 1.5)
    norm_bias = scatter_about(keys[11], (D,), 0.3, 2.0, jnp.float32)
    proj_weight = scatter_about(keys[12], (D, EMB), D ** -0.5, 0.21875)
    return {"query_states": query_states, "passage_states": passage_states, "query_lengths": query_lengths, "passage_lengths": passage_lengths, "passage_ids": passage_ids, "positives": positives, "up_weight": up_weight, "up_bias": up_bias, "down_weight": down_weight, "down_bias": down_bias, "norm_gain": norm_gain, "norm_bias": norm_bias, "proj_weight": proj_weight}


temper = 0.05
eps_norm = 1e-06
punct_low = 999
punct_high = 1067

def encode_rows(token_rows, up_weight, up_bias, down_weight, down_bias, norm_gain, norm_bias, proj_weight):
    upward = jnp.dot(token_rows, up_weight, preferred_element_type=jnp.float32) + up_bias
    activated = jax.nn.gelu(upward, approximate=False).astype(jnp.bfloat16)
    residual = token_rows.astype(jnp.float32) + jnp.dot(activated, down_weight, preferred_element_type=jnp.float32) + down_bias
    average = lax.optimization_barrier(jnp.mean(residual, -1, keepdims=True))
    centered = residual - average
    variance = lax.optimization_barrier(jnp.mean(centered * centered, -1, keepdims=True))
    hidden = (centered * lax.rsqrt(variance + eps_norm) * norm_gain + norm_bias).astype(jnp.bfloat16)
    projected = jnp.dot(hidden, proj_weight, preferred_element_type=jnp.float32)
    inverse = lax.rsqrt(lax.optimization_barrier(jnp.sum(projected * projected, -1, keepdims=True)) + eps_norm)
    return (hidden, projected * inverse, inverse)

def token_scores(query_flat, query_keep, block_emb, block_keep, query_count):
    item_count, pass_len, embed_dim = block_emb.shape
    similar = jnp.dot(query_flat, block_emb.reshape(item_count * pass_len, embed_dim).T, preferred_element_type=jnp.float32)
    weights = jnp.exp(similar / temper).reshape(-1, item_count, pass_len) * block_keep.astype(jnp.float32)[None]
    totals = lax.optimization_barrier(jnp.sum(weights, -1))
    soft_max = temper * jnp.log(totals) * query_keep[:, None]
    scores = lax.optimization_barrier(jnp.sum(soft_max.reshape(query_count, -1, item_count), 1))
    return (scores, weights, totals)

def token_grads(query_flat, query_keep, block_emb, weights, totals, dscore, query_count):
    item_count, pass_len, embed_dim = block_emb.shape
    factor = (dscore[:, None, :] * query_keep.reshape(query_count, -1)[:, :, None]).reshape(-1, item_count) / totals
    sim_grad = (weights * factor[:, :, None]).reshape(-1, item_count * pass_len).astype(jnp.bfloat16)
    passage_term = jnp.dot(sim_grad.T, query_flat, preferred_element_type=jnp.float32)
    query_term = jnp.dot(sim_grad, block_emb.reshape(item_count * pass_len, embed_dim), preferred_element_type=jnp.float32)
    return (passage_term.reshape(item_count, pass_len, embed_dim), query_term)

def cross_entropy(scores, positives):
    log_total = jnp.log(lax.optimization_barrier(jnp.sum(jnp.exp(scores), 1)))
    onehot = (jnp.arange(scores.shape[1], dtype=jnp.int32)[None, :] == positives[:, None]).astype(jnp.float32)
    loss_sum = jnp.sum(log_total - lax.optimization_barrier(jnp.sum(scores * onehot, 1)))
    dscore = jnp.exp(scores - log_total[:, None]) - onehot
    return (loss_sum, dscore)

def norm_backward(gradient, normed, inverse):
    return (inverse * (gradient - normed * lax.optimization_barrier(jnp.sum(normed * gradient, -1, keepdims=True)))).astype(jnp.bfloat16)

def reference(query_states, passage_states, query_lengths, passage_lengths, passage_ids, positives, up_weight, up_bias, down_weight, down_bias, norm_gain, norm_bias, proj_weight):

    def encode_all(states, per_block):
        item_count, length, model_width = states.shape
        blocks = states.reshape(item_count // per_block, per_block * length, model_width)

        def encode_block(block):
            return encode_rows(block, up_weight, up_bias, down_weight, down_bias, norm_gain, norm_bias, proj_weight)
        hidden, normed, inverse = lax.map(encode_block, blocks)
        return (hidden.reshape(-1, model_width), normed.reshape(-1, EMB), inverse.reshape(-1, 1))
    query_hidden, query_normed, query_inverse = encode_all(query_states, Q_DEV)
    pass_hidden, pass_normed, pass_inverse = encode_all(passage_states, P_DEV)
    query_emb = query_normed.astype(jnp.bfloat16).reshape(N_REP, N_DP, Q_DEV * QLEN, EMB)
    query_keep = (jnp.arange(QLEN, dtype=jnp.int32)[None, :] < query_lengths[:, None]).astype(jnp.float32)
    query_keep = query_keep.reshape(N_REP, N_DP, Q_DEV * QLEN)
    is_punct = (passage_ids >= punct_low) & (passage_ids < punct_high)
    pass_keep = ((jnp.arange(PLEN, dtype=jnp.int32)[None, :] < passage_lengths[:, None]) & jnp.logical_not(is_punct)).astype(jnp.float32)
    pass_keep = pass_keep.reshape(N_REP, GROUP_P, PLEN)
    pass_emb = pass_normed.astype(jnp.bfloat16).reshape(N_REP, GROUP_P, PLEN, EMB)
    grouped_pos = positives.reshape(N_REP, N_DP, Q_DEV)

    def one_group(operands):
        group_query, group_qkeep, group_pass, group_pkeep, group_pos = operands

        def advance(pass_grad, block):
            block_query, block_keep, block_pos = block
            scores, weights, totals = token_scores(block_query, block_keep, group_pass, group_pkeep, Q_DEV)
            loss_sum, dscore = cross_entropy(scores, block_pos)
            passage_term, query_term = token_grads(block_query, block_keep, group_pass, weights, totals, dscore, Q_DEV)
            return (pass_grad + passage_term, (loss_sum, query_term))
        start_grad = jnp.zeros((GROUP_P, PLEN, EMB), jnp.float32)
        pass_grad, (losses, query_terms) = lax.scan(advance, start_grad, (group_query, group_qkeep, group_pos))
        return (pass_grad, jnp.sum(losses), query_terms)
    pass_grad, losses, query_grad = lax.map(one_group, (query_emb, query_keep, pass_emb, pass_keep, grouped_pos))
    passage_grad = pass_grad.reshape(PASSAGES, PLEN, EMB)
    mean_loss = jnp.sum(losses) / QUERIES
    query_back = norm_backward(query_grad.reshape(-1, EMB), query_normed, query_inverse)
    pass_back = norm_backward(passage_grad.reshape(-1, EMB), pass_normed, pass_inverse)
    proj_grad = jnp.dot(query_hidden.T, query_back, preferred_element_type=jnp.float32) + jnp.dot(pass_hidden.T, pass_back, preferred_element_type=jnp.float32)
    return (mean_loss, passage_grad, proj_grad)
```

```python
import functools

import jax
import jax.numpy as jnp
from jax import lax
from jax.experimental import pallas as pl
from jax.experimental.pallas import tpu as pltpu
from jax.sharding import PartitionSpec as P

MESH = pl.DeviceIdType.MESH

temper = 0.05
eps_norm = 1e-06
punct_low = 999
punct_high = 1067


def encode_rows(
    token_rows, up_weight, up_bias, down_weight, down_bias, norm_gain, norm_bias, proj_weight
):
    upward = jnp.dot(token_rows, up_weight, preferred_element_type=jnp.float32) + up_bias
    activated = jax.nn.gelu(upward, approximate=False).astype(jnp.bfloat16)
    residual = (
        token_rows.astype(jnp.float32)
        + jnp.dot(activated, down_weight, preferred_element_type=jnp.float32)
        + down_bias
    )
    average = jnp.mean(residual, -1, keepdims=True)
    centered = residual - average
    variance = jnp.mean(centered * centered, -1, keepdims=True)
    hidden = (centered * lax.rsqrt(variance + eps_norm) * norm_gain + norm_bias).astype(
        jnp.bfloat16
    )
    projected = jnp.dot(hidden, proj_weight, preferred_element_type=jnp.float32)
    inverse = lax.rsqrt(jnp.sum(projected * projected, -1, keepdims=True) + eps_norm)
    return (hidden, projected * inverse, inverse)


def greet(axes):
    barrier = pltpu.get_barrier_semaphore()
    count = 0
    for axis in axes:
        size = lax.axis_size(axis)
        me = lax.axis_index(axis)
        for off in range(1, size):
            pl.semaphore_signal(
                barrier, inc=1, device_id={axis: lax.rem(me + off, size)}, device_id_type=MESH
            )
        count += size - 1
    pl.semaphore_wait(barrier, count)


def send_all(axis, source, target, send_sem, recv_sem):
    size = lax.axis_size(axis)
    me = lax.axis_index(axis)
    copies = []
    for off in range(1, size):
        peer = lax.rem(me + off, size)
        copy = pltpu.make_async_remote_copy(
            src_ref=source(peer),
            dst_ref=target.at[me],
            send_sem=send_sem.at[off - 1],
            recv_sem=recv_sem.at[off - 1],
            device_id={axis: peer},
            device_id_type=MESH,
        )
        copy.start()
        copies.append(copy)
    return copies


def gather_kernel(*refs):
    count = len(refs) // 4
    sources, targets = refs[:count], refs[count : 2 * count]
    sems = refs[2 * count :]
    greet(("dp",))
    me = lax.axis_index("dp")
    copies = []
    for k in range(count):
        copies += send_all(
            "dp", lambda peer: sources[k], targets[k], sems[2 * k], sems[2 * k + 1]
        )
    for k in range(count):
        targets[k][me] = sources[k][...]
    for copy in copies:
        copy.wait()


def comm_params(collective_id):
    return pltpu.CompilerParams(collective_id=collective_id, has_side_effects=True)


def gather_dp(arrays, collective_id):
    size = lax.axis_size("dp")
    vmem = pl.BlockSpec(memory_space=pltpu.VMEM)
    return pl.pallas_call(
        gather_kernel,
        out_shape=[jax.ShapeDtypeStruct((size,) + a.shape, a.dtype) for a in arrays],
        in_specs=[vmem] * len(arrays),
        out_specs=[vmem] * len(arrays),
        scratch_shapes=[pltpu.SemaphoreType.DMA((size - 1,))] * (2 * len(arrays)),
        compiler_params=comm_params(collective_id),
    )(*arrays)


def scatter_kernel(parts, out, landed, send_sem, recv_sem):
    greet(("dp",))
    me = lax.axis_index("dp")
    copies = send_all("dp", lambda peer: parts.at[peer], landed, send_sem, recv_sem)
    landed[me] = parts[me]
    for copy in copies:
        copy.wait()
    total = landed[0].astype(jnp.float32)
    for k in range(1, lax.axis_size("dp")):
        total = total + landed[k].astype(jnp.float32)
    out[...] = total


def scatter_dp(parts, collective_id):
    size = lax.axis_size("dp")
    vmem = pl.BlockSpec(memory_space=pltpu.VMEM)
    return pl.pallas_call(
        scatter_kernel,
        out_shape=jax.ShapeDtypeStruct(parts.shape[1:], jnp.float32),
        in_specs=[vmem],
        out_specs=vmem,
        scratch_shapes=[pltpu.VMEM(parts.shape, parts.dtype)]
        + [pltpu.SemaphoreType.DMA((size - 1,))] * 2,
        compiler_params=comm_params(collective_id),
    )(parts)


def reduce_kernel(
    parts, loss, out, loss_out, landed, crossed, summed, full, s1, r1, s2, r2, s3, r3
):
    greet(("dp", "rep"))
    me = lax.axis_index("dp")
    mine = lax.axis_index("rep")
    rows = parts.shape[1]
    copies = send_all("dp", lambda peer: parts.at[peer], landed, s1, r1)
    landed[me] = parts[me]
    for copy in copies:
        copy.wait()
    total = landed[0].astype(jnp.float32)
    for k in range(1, lax.axis_size("dp")):
        total = total + landed[k].astype(jnp.float32)
    summed[0:rows] = total
    summed[rows:] = loss[...]
    copies = send_all("rep", lambda peer: summed, crossed, s2, r2)
    crossed[mine] = summed[...]
    for copy in copies:
        copy.wait()
    total = crossed[0]
    for k in range(1, lax.axis_size("rep")):
        total = total + crossed[k]
    loss_out[...] = total[rows:]
    full[me] = total[0:rows].astype(full.dtype)
    copies = send_all("dp", lambda peer: full.at[me], full, s3, r3)
    for copy in copies:
        copy.wait()
    out[...] = full[...].astype(jnp.float32)


def reduce_all(parts, loss, collective_id):
    size, reps = lax.axis_size("dp"), lax.axis_size("rep")
    rows, lanes = parts.shape[1:]
    vmem = pl.BlockSpec(memory_space=pltpu.VMEM)
    extra = loss.shape[0]
    return pl.pallas_call(
        reduce_kernel,
        out_shape=[
            jax.ShapeDtypeStruct(parts.shape, jnp.float32),
            jax.ShapeDtypeStruct(loss.shape, jnp.float32),
        ],
        in_specs=[vmem] * 2,
        out_specs=[vmem] * 2,
        scratch_shapes=[
            pltpu.VMEM(parts.shape, parts.dtype),
            pltpu.VMEM((reps, rows + extra, lanes), jnp.float32),
            pltpu.VMEM((rows + extra, lanes), jnp.float32),
            pltpu.VMEM(parts.shape, parts.dtype),
        ]
        + [pltpu.SemaphoreType.DMA((size - 1,))] * 2
        + [pltpu.SemaphoreType.DMA((reps - 1,))] * 2
        + [pltpu.SemaphoreType.DMA((size - 1,))] * 2,
        compiler_params=comm_params(collective_id),
    )(parts, loss)


def norm_backward(gradient, normed, inverse):
    return (inverse * (gradient - normed * jnp.sum(normed * gradient, -1, keepdims=True))).astype(
        jnp.bfloat16
    )


def tile_rows(array):
    return jnp.pad(array, ((0, -array.shape[0] % 8), (0, -array.shape[1] % 128)))


def per_device(
    query_states,
    passage_states,
    query_lengths,
    passage_lengths,
    passage_ids,
    positives,
    up_weight,
    up_bias,
    down_weight,
    down_bias,
    norm_gain,
    norm_bias,
    proj_weight,
):
    query_count, query_len, model_width = query_states.shape
    pass_count, pass_len, _ = passage_states.shape
    embed_dim = proj_weight.shape[1]
    groups = lax.axis_size("dp")
    token_rows = jnp.concatenate(
        [query_states.reshape(-1, model_width), passage_states.reshape(-1, model_width)], 0
    )
    hidden, normed, inverse = encode_rows(
        token_rows, up_weight, up_bias, down_weight, down_bias, norm_gain, norm_bias, proj_weight
    )
    boundary = query_count * query_len
    query_emb = normed[:boundary].astype(jnp.bfloat16)
    pass_emb = normed[boundary:].astype(jnp.bfloat16).reshape(pass_count, pass_len, embed_dim)
    is_punct = (passage_ids >= punct_low) & (passage_ids < punct_high)
    pass_keep = (
        (jnp.arange(pass_len, dtype=jnp.int32)[None, :] < passage_lengths[:, None])
        & jnp.logical_not(is_punct)
    ).astype(jnp.float32)

    facts = tile_rows(jnp.stack([query_lengths, positives]))
    all_emb, all_facts = gather_dp((query_emb, facts), 1)
    all_emb = all_emb.reshape(-1, embed_dim)
    all_lengths = all_facts[:, 0, :query_count].reshape(-1)
    all_positives = all_facts[:, 1, :query_count].reshape(-1)
    group_count = query_count * groups
    query_keep = (
        jnp.arange(query_len, dtype=jnp.int32)[None, :] < all_lengths[:, None]
    ).astype(jnp.float32)

    weights, totals = [], []
    for p in range(pass_count):
        similar = lax.dot_general(
            all_emb, pass_emb[p], (((1,), (1,)), ((), ())), preferred_element_type=jnp.float32
        )
        weight = jnp.exp(similar / temper) * pass_keep[p][None]
        weights.append(weight)
        totals.append(jnp.sum(weight, -1).reshape(group_count, query_len))
    scores = jnp.stack(
        [jnp.sum(temper * jnp.log(total) * query_keep, 1) for total in totals], 1
    )
    first = lax.axis_index("dp") * pass_count
    onehot = (
        first + jnp.arange(pass_count, dtype=jnp.int32)[None, :] == all_positives[:, None]
    ).astype(jnp.float32)
    shares = tile_rows(jnp.stack([jnp.sum(jnp.exp(scores), 1), jnp.sum(scores * onehot, 1)]))
    (all_shares,) = gather_dp((shares,), 2)
    both = jnp.sum(all_shares, 0)
    log_total = jnp.log(both[0, :group_count])
    loss_sum = jnp.sum(log_total - both[1, :group_count])
    dscore = jnp.exp(scores - log_total[:, None]) - onehot

    pass_terms = []
    query_part = None
    for p in range(pass_count):
        factor = (dscore[:, p : p + 1] * query_keep / totals[p]).reshape(-1, 1)
        sim_grad = (weights[p] * factor).astype(jnp.bfloat16)
        pass_terms.append(
            lax.dot_general(
                sim_grad, all_emb, (((0,), (0,)), ((), ())), preferred_element_type=jnp.float32
            )
        )
        term = jnp.dot(sim_grad, pass_emb[p], preferred_element_type=jnp.float32)
        query_part = term if query_part is None else query_part + term
    passage_grad = jnp.stack(pass_terms)
    query_grad = scatter_dp(
        query_part.astype(jnp.bfloat16).reshape(groups, boundary, embed_dim), 3
    )
    query_back = norm_backward(query_grad, normed[:boundary], inverse[:boundary])
    pass_back = norm_backward(
        passage_grad.reshape(-1, embed_dim), normed[boundary:], inverse[boundary:]
    )
    all_back = jnp.concatenate([query_back, pass_back], 0)
    local_sum = lax.dot_general(
        hidden, all_back, (((0,), (0,)), ((), ())), preferred_element_type=jnp.float32
    )
    proj_total, loss_total = reduce_all(
        local_sum.astype(jnp.bfloat16).reshape(groups, -1, embed_dim),
        jnp.full((8, 128), loss_sum, jnp.float32),
        4,
    )
    mean_loss = loss_total[0, 0] / (group_count * lax.axis_size("rep"))
    return (mean_loss, passage_grad, proj_total.reshape(model_width, embed_dim))


def solution(mesh):
    in_specs = (
        P(("rep", "dp"), None, None),
        P(("rep", "dp"), None, None),
        P(("rep", "dp")),
        P(("rep", "dp")),
        P(("rep", "dp"), None),
        P(("rep", "dp")),
        P(),
        P(),
        P(),
        P(),
        P(),
        P(),
        P(),
    )
    out_specs = (P(), P(("rep", "dp"), None, None), P())
    return jax.shard_map(
        per_device, mesh=mesh, in_specs=in_specs, out_specs=out_specs, check_vma=False
    )
```

```python
import functools

import jax
import jax.numpy as jnp
from jax import lax
from jax.experimental import pallas as pl
from jax.experimental.pallas import tpu as pltpu
from jax.sharding import PartitionSpec as P

MESH = pl.DeviceIdType.MESH

temper = 0.05
eps_norm = 1e-06
punct_low = 999
punct_high = 1067


erf_top = (
    -2.72614225801306e-10,
    2.77068142495902e-08,
    -2.10102402082508e-06,
    -5.69250639462346e-05,
    -7.34990630326855e-04,
    -2.95459980854025e-03,
    -1.60960333262415e-02,
)
erf_low = (
    -1.45660718464996e-05,
    -2.13374055278905e-04,
    -1.68282697438203e-03,
    -7.37332916720468e-03,
    -1.42647390514189e-02,
)
row_tile = 256
unit_tile = 512


def erf(value):
    value = jnp.clip(value, -4.0, 4.0)
    square = value * value
    top = square * erf_top[0] + erf_top[1]
    for factor in erf_top[2:]:
        top = top * square + factor
    low = square * erf_low[0] + erf_low[1]
    for factor in erf_low[2:]:
        low = low * square + factor
    return value * top / low


def encode_kernel(
    rows, up, up_bias, down, down_bias, gain, bias, proj, hidden, normed, inverse, total
):
    step = pl.program_id(0)

    def tile(k, carry):
        here = pl.ds(pl.multiple_of(k * row_tile, row_tile), row_tile)
        block = rows[here, :]

        @pl.when(step == 0)
        def _():
            total[here, :] = block.astype(jnp.float32) + down_bias[...]

        upward = jnp.dot(block, up[...], preferred_element_type=jnp.float32) + up_bias[...]
        activated = (0.5 * upward * (1.0 + erf(upward * (0.5**0.5)))).astype(jnp.bfloat16)
        total[here, :] += jnp.dot(activated, down[...], preferred_element_type=jnp.float32)

        @pl.when(step == pl.num_programs(0) - 1)
        def _():
            residual = total[here, :]
            centered = residual - jnp.mean(residual, -1, keepdims=True)
            variance = jnp.mean(centered * centered, -1, keepdims=True)
            kept = (centered * lax.rsqrt(variance + eps_norm) * gain[...] + bias[...]).astype(
                jnp.bfloat16
            )
            hidden[here, :] = kept
            projected = jnp.dot(kept, proj[...], preferred_element_type=jnp.float32)
            scale = lax.rsqrt(jnp.sum(projected * projected, -1, keepdims=True) + eps_norm)
            normed[here, :] = projected * scale
            inverse[here, :] = jnp.broadcast_to(scale, projected.shape)

        return carry

    lax.fori_loop(0, rows.shape[0] // row_tile, tile, 0)


def encode_rows(
    token_rows, up_weight, up_bias, down_weight, down_bias, norm_gain, norm_bias, proj_weight
):
    count, width = token_rows.shape
    units, embed = up_weight.shape[1], proj_weight.shape[1]

    def whole(*shape):
        return pl.BlockSpec(shape, lambda c: (0, 0))

    return pl.pallas_call(
        encode_kernel,
        grid=(units // unit_tile,),
        in_specs=[
            whole(count, width),
            pl.BlockSpec((width, unit_tile), lambda c: (0, c)),
            pl.BlockSpec((1, unit_tile), lambda c: (0, c)),
            pl.BlockSpec((unit_tile, width), lambda c: (c, 0)),
            whole(1, width),
            whole(1, width),
            whole(1, width),
            whole(width, embed),
        ],
        out_specs=[whole(count, width), whole(count, embed), whole(count, embed)],
        out_shape=[
            jax.ShapeDtypeStruct((count, width), jnp.bfloat16),
            jax.ShapeDtypeStruct((count, embed), jnp.float32),
            jax.ShapeDtypeStruct((count, embed), jnp.float32),
        ],
        scratch_shapes=[pltpu.VMEM((count, width), jnp.float32)],
        compiler_params=pltpu.CompilerParams(dimension_semantics=("arbitrary",)),
        cost_estimate=pl.CostEstimate(
            flops=4 * count * width * units,
            bytes_accessed=8 * width * units,
            transcendentals=count * units,
        ),
    )(
        token_rows,
        up_weight,
        up_bias[None],
        down_weight,
        down_bias[None],
        norm_gain[None],
        norm_bias[None],
        proj_weight,
    )


def greet(axes):
    barrier = pltpu.get_barrier_semaphore()
    count = 0
    for axis in axes:
        size = lax.axis_size(axis)
        me = lax.axis_index(axis)
        for off in range(1, size):
            pl.semaphore_signal(
                barrier, inc=1, device_id={axis: lax.rem(me + off, size)}, device_id_type=MESH
            )
        count += size - 1
    pl.semaphore_wait(barrier, count)


def send_all(axis, source, target, send_sem, recv_sem):
    size = lax.axis_size(axis)
    me = lax.axis_index(axis)
    copies = []
    for off in range(1, size):
        peer = lax.rem(me + off, size)
        copy = pltpu.make_async_remote_copy(
            src_ref=source(peer),
            dst_ref=target.at[me],
            send_sem=send_sem.at[off - 1],
            recv_sem=recv_sem.at[off - 1],
            device_id={axis: peer},
            device_id_type=MESH,
        )
        copy.start()
        copies.append(copy)
    return copies


def gather_kernel(*refs):
    count = len(refs) // 4
    sources, targets = refs[:count], refs[count : 2 * count]
    sems = refs[2 * count :]
    greet(("dp",))
    me = lax.axis_index("dp")
    copies = []
    for k in range(count):
        copies += send_all(
            "dp", lambda peer: sources[k], targets[k], sems[2 * k], sems[2 * k + 1]
        )
    for k in range(count):
        targets[k][me] = sources[k][...]
    for copy in copies:
        copy.wait()


def comm_params(collective_id):
    return pltpu.CompilerParams(collective_id=collective_id, has_side_effects=True)


def gather_dp(arrays, collective_id):
    size = lax.axis_size("dp")
    vmem = pl.BlockSpec(memory_space=pltpu.VMEM)
    return pl.pallas_call(
        gather_kernel,
        out_shape=[jax.ShapeDtypeStruct((size,) + a.shape, a.dtype) for a in arrays],
        in_specs=[vmem] * len(arrays),
        out_specs=[vmem] * len(arrays),
        scratch_shapes=[pltpu.SemaphoreType.DMA((size - 1,))] * (2 * len(arrays)),
        compiler_params=comm_params(collective_id),
    )(*arrays)


def scatter_kernel(parts, out, landed, send_sem, recv_sem):
    greet(("dp",))
    me = lax.axis_index("dp")
    size = lax.axis_size("dp")
    copies = send_all("dp", lambda peer: parts.at[lax.rem(me - peer + size, size)], landed, send_sem, recv_sem)
    landed[me] = parts[0]
    for copy in copies:
        copy.wait()
    total = landed[0].astype(jnp.float32)
    for k in range(1, lax.axis_size("dp")):
        total = total + landed[k].astype(jnp.float32)
    out[...] = total


def scatter_dp(parts, collective_id):
    size = lax.axis_size("dp")
    vmem = pl.BlockSpec(memory_space=pltpu.VMEM)
    return pl.pallas_call(
        scatter_kernel,
        out_shape=jax.ShapeDtypeStruct(parts.shape[1:], jnp.float32),
        in_specs=[vmem],
        out_specs=vmem,
        scratch_shapes=[pltpu.VMEM(parts.shape, parts.dtype)]
        + [pltpu.SemaphoreType.DMA((size - 1,))] * 2,
        compiler_params=comm_params(collective_id),
    )(parts)


def reduce_kernel(
    parts, loss, out, loss_out, landed, crossed, summed, full, s1, r1, s2, r2, s3, r3
):
    greet(("dp", "rep"))
    me = lax.axis_index("dp")
    mine = lax.axis_index("rep")
    rows = parts.shape[1]
    copies = send_all("dp", lambda peer: parts.at[peer], landed, s1, r1)
    landed[me] = parts[me]
    for copy in copies:
        copy.wait()
    total = landed[0].astype(jnp.float32)
    for k in range(1, lax.axis_size("dp")):
        total = total + landed[k].astype(jnp.float32)
    summed[0:rows] = total
    summed[rows:] = loss[...]
    copies = send_all("rep", lambda peer: summed, crossed, s2, r2)
    crossed[mine] = summed[...]
    for copy in copies:
        copy.wait()
    total = crossed[0]
    for k in range(1, lax.axis_size("rep")):
        total = total + crossed[k]
    loss_out[...] = total[rows:]
    full[me] = total[0:rows].astype(full.dtype)
    copies = send_all("dp", lambda peer: full.at[me], full, s3, r3)
    for copy in copies:
        copy.wait()
    out[...] = full[...].astype(jnp.float32)


def reduce_all(parts, loss, collective_id):
    size, reps = lax.axis_size("dp"), lax.axis_size("rep")
    rows, lanes = parts.shape[1:]
    vmem = pl.BlockSpec(memory_space=pltpu.VMEM)
    extra = loss.shape[0]
    return pl.pallas_call(
        reduce_kernel,
        out_shape=[
            jax.ShapeDtypeStruct(parts.shape, jnp.float32),
            jax.ShapeDtypeStruct(loss.shape, jnp.float32),
        ],
        in_specs=[vmem] * 2,
        out_specs=[vmem] * 2,
        scratch_shapes=[
            pltpu.VMEM(parts.shape, parts.dtype),
            pltpu.VMEM((reps, rows + extra, lanes), jnp.float32),
            pltpu.VMEM((rows + extra, lanes), jnp.float32),
            pltpu.VMEM(parts.shape, parts.dtype),
        ]
        + [pltpu.SemaphoreType.DMA((size - 1,))] * 2
        + [pltpu.SemaphoreType.DMA((reps - 1,))] * 2
        + [pltpu.SemaphoreType.DMA((size - 1,))] * 2,
        compiler_params=comm_params(collective_id),
    )(parts, loss)


def norm_backward(gradient, normed, inverse):
    return (inverse * (gradient - normed * jnp.sum(normed * gradient, -1, keepdims=True))).astype(
        jnp.bfloat16
    )


def tile_rows(array):
    return jnp.pad(array, ((0, -array.shape[0] % 8), (0, -array.shape[1] % 128)))


def per_device(
    query_states,
    passage_states,
    query_lengths,
    passage_lengths,
    passage_ids,
    positives,
    up_weight,
    up_bias,
    down_weight,
    down_bias,
    norm_gain,
    norm_bias,
    proj_weight,
):
    query_count, query_len, model_width = query_states.shape
    pass_count, pass_len, _ = passage_states.shape
    embed_dim = proj_weight.shape[1]
    groups = lax.axis_size("dp")
    boundary = query_count * query_len
    finish = pass_count * pass_len
    params = (up_weight, up_bias, down_weight, down_bias, norm_gain, norm_bias, proj_weight)

    def encode(states):
        rows = states.reshape(-1, model_width)
        return encode_rows(jnp.pad(rows, ((0, -rows.shape[0] % row_tile), (0, 0))), *params)

    query_hidden, query_normed, query_inverse = encode(query_states)
    facts = jnp.pad(
        jnp.stack([query_lengths, positives]).astype(jnp.bfloat16),
        ((0, 14), (0, embed_dim - query_count)),
    )
    parcel = jnp.concatenate([query_normed[:boundary].astype(jnp.bfloat16), facts], 0)
    parcels = [parcel]
    for off in range(1, groups):
        ring = [(k, (k + off) % groups) for k in range(groups)]
        parcels.append(lax.ppermute(parcel, "dp", ring))
    pass_hidden, pass_normed, pass_inverse = encode(passage_states)
    pass_emb = pass_normed[:finish].astype(jnp.bfloat16).reshape(pass_count, pass_len, embed_dim)
    is_punct = (passage_ids >= punct_low) & (passage_ids < punct_high)
    pass_keep = (
        (jnp.arange(pass_len, dtype=jnp.int32)[None, :] < passage_lengths[:, None])
        & jnp.logical_not(is_punct)
    ).astype(jnp.float32)

    all_emb = jnp.concatenate([block[:boundary] for block in parcels], 0)
    all_facts = jnp.stack([block[boundary : boundary + 2, :query_count] for block in parcels])
    all_facts = all_facts.astype(jnp.int32)
    all_lengths = all_facts[:, 0].reshape(-1)
    all_positives = all_facts[:, 1].reshape(-1)
    me = lax.axis_index("dp")
    steps = jnp.arange(groups, dtype=jnp.int32)
    swap = (me - steps[:, None] + groups) % groups == steps[None, :]

    def swapped(values):
        blocks = values.reshape(-1, 1, groups, query_count)
        return jnp.sum(jnp.where(swap[None, :, :, None], blocks, 0.0), 2).reshape(values.shape)

    group_count = query_count * groups
    query_keep = (
        jnp.arange(query_len, dtype=jnp.int32)[None, :] < all_lengths[:, None]
    ).astype(jnp.float32)

    weights, totals = [], []
    for p in range(pass_count):
        similar = lax.dot_general(
            all_emb, pass_emb[p], (((1,), (1,)), ((), ())), preferred_element_type=jnp.float32
        )
        weight = jnp.exp(similar / temper) * pass_keep[p][None]
        weights.append(weight)
        totals.append(jnp.sum(weight, -1).reshape(group_count, query_len))
    scores = jnp.stack(
        [jnp.sum(temper * jnp.log(total) * query_keep, 1) for total in totals], 1
    )
    first = lax.axis_index("dp") * pass_count
    onehot = (
        first + jnp.arange(pass_count, dtype=jnp.int32)[None, :] == all_positives[:, None]
    ).astype(jnp.float32)
    shares = jnp.stack([jnp.sum(jnp.exp(scores), 1), jnp.sum(scores * onehot, 1)])
    shares = tile_rows(swapped(shares))
    (all_shares,) = gather_dp((shares,), 2)
    both = jnp.sum(all_shares, 0)
    log_total = jnp.log(both[0, :group_count])
    loss_sum = jnp.sum(log_total - both[1, :group_count])
    dscore = jnp.exp(scores - swapped(log_total)[:, None]) - onehot

    pass_terms = []
    query_part = None
    for p in range(pass_count):
        factor = (dscore[:, p : p + 1] * query_keep / totals[p]).reshape(-1, 1)
        sim_grad = (weights[p] * factor).astype(jnp.bfloat16)
        pass_terms.append(
            lax.dot_general(
                sim_grad, all_emb, (((0,), (0,)), ((), ())), preferred_element_type=jnp.float32
            )
        )
        term = jnp.dot(sim_grad, pass_emb[p], preferred_element_type=jnp.float32)
        query_part = term if query_part is None else query_part + term
    passage_grad = jnp.stack(pass_terms)
    query_grad = scatter_dp(
        query_part.astype(jnp.bfloat16).reshape(groups, boundary, embed_dim), 3
    )
    query_back = norm_backward(query_grad, query_normed[:boundary], query_inverse[:boundary])
    pass_back = norm_backward(
        passage_grad.reshape(-1, embed_dim), pass_normed[:finish], pass_inverse[:finish]
    )

    def outer(hidden, back):
        back = jnp.pad(back, ((0, hidden.shape[0] - back.shape[0]), (0, 0)))
        return lax.dot_general(
            hidden, back, (((0,), (0,)), ((), ())), preferred_element_type=jnp.float32
        )

    local_sum = outer(query_hidden, query_back) + outer(pass_hidden, pass_back)
    proj_total, loss_total = reduce_all(
        local_sum.astype(jnp.bfloat16).reshape(groups, -1, embed_dim),
        jnp.full((8, 128), loss_sum, jnp.float32),
        4,
    )
    mean_loss = loss_total[0, 0] / (group_count * lax.axis_size("rep"))
    return (mean_loss, passage_grad, proj_total.reshape(model_width, embed_dim))


def solution(mesh):
    in_specs = (
        P(("rep", "dp"), None, None),
        P(("rep", "dp"), None, None),
        P(("rep", "dp")),
        P(("rep", "dp")),
        P(("rep", "dp"), None),
        P(("rep", "dp")),
        P(),
        P(),
        P(),
        P(),
        P(),
        P(),
        P(),
    )
    out_specs = (P(), P(("rep", "dp"), None, None), P())
    return jax.shard_map(
        per_device, mesh=mesh, in_specs=in_specs, out_specs=out_specs, check_vma=False
    )
```
